256 devices in a mesh: tx: 4 (over x_hi, core), ty: 8 (over z), src: 8 (over y, x_lo).
Axes of the slice: x: 4 (x_hi: 2, x_lo: 2; x = x_hi * 2 + x_lo), y: 4, z: 8, core: 2. Of those that a mesh axis runs over, the one named last changes fastest.
Arguments:
- spectrum: bfloat16 [2, 512, 512], P(None, ('tx', 'ty'), 'src'), may hold values from -0.0234375 to 0.0234375
- pupil_mask: int32 [256, 256], replicated, may hold values 0 or 1
- source_shifts: int32 [256, 2], P('src'), may hold values from 0 to 256
- source_weights: int32 [256], P('src'), may hold values from 0 to 8, as said below
Outputs:
- acid_level: float32 [2048, 2048], P(('tx', 'src'), 'ty')
The draws below stay inside these ranges and needn't reach their ends.
Inputs may be any that keep to these rules, and one draw needn't show every extreme that they name: `source_weights`: the 32 consecutive sources of each group (one index of src) hold at least 4 points with weight above 0; some group has all 32 points on.
All inputs are finite; a program needn't handle non-finite values.
Results may differ from the reference program's by a relative error of at most 0.0017.
Values may be sent and summed in bfloat16 or wider, within the bound.
No kernel may reach another device: no remote copies, remote signals or barrier semaphores. Data moves between devices by JAX's collectives and lax.ppermute only.
A program may use at most 64 MiB of HBM per device.

```python
import jax
import jax.numpy as jnp
from jax import lax

K = 256
MW = 512
FRAME = 2048
SRC_DEV = 32
SOURCES = 256
NX = 2048
NY = 2048


def slot_order(subkey):
    return jax.random.permutation(subkey, SRC_DEV)


def draw_source_weights(key, part):
    group_count = SOURCES // SRC_DEV
    subkeys = jax.random.split(jax.random.fold_in(key, 11), 4)
    counts = jax.random.randint(subkeys[0], (group_count,), SRC_DEV // 8, SRC_DEV // 2 + 1)
    full_group = jax.random.randint(subkeys[1], (), 0, group_count)
    counts = jnp.where(jnp.arange(group_count) == full_group, SRC_DEV, counts)
    slot_rank = jax.vmap(slot_order)(jax.random.split(subkeys[2], group_count))
    levels = jax.random.randint(subkeys[3], (group_count, SRC_DEV), 1, 9)
    levels = levels.at[full_group, 0].set(8)
    chosen = jnp.where(slot_rank < counts[:, None], levels, 0)
    return chosen.reshape(SOURCES).astype(jnp.int32)


def touch_ends(values, key, low, top_value):
    longest = values.shape.index(max(values.shape))
    spots = []
    for shift in (0, 1):
        where = [jax.random.randint(jax.random.fold_in(key, axis), (), 0, length) for axis, length in enumerate(values.shape)]
        where[longest] = (where[longest] + shift) % values.shape[longest]
        spots.append(tuple(where))
    return values.at[spots[0]].set(low).at[spots[1]].set(top_value)


def block_scale(key, dims, shards, least, high):
    factor_of = 1.0
    for dim, parts in shards:
        steps = jax.random.uniform(jax.random.fold_in(jax.random.fold_in(key, 6), dim), (parts,), jnp.float32, least / len(shards), high / len(shards))
        factor_of = factor_of * jnp.repeat(jnp.exp(steps), dims[dim] // parts).reshape((-1,) + (1,) * (len(dims) - 1 - dim))
    return factor_of


def centred(stream_key, shape, spread, most, cuts=(), kind=jnp.bfloat16):
    level = block_scale(stream_key, shape, cuts, -0.22, 0.18) if cuts else 1.0
    entries = jax.random.normal(stream_key, shape, jnp.float32) * spread * level
    return jnp.minimum(jnp.maximum(entries, -most), most).astype(kind)


def setup_inputs(seed: int = 0) -> dict:
    splits = jax.random.split(jax.random.key(seed), 5)
    return {
        "spectrum": centred(splits[0], (2, MW, MW), (K * K) ** -0.5, 0.0234375, ((1, 32), (2, 8))),
        "pupil_mask": touch_ends((jax.random.randint(splits[1], (K, K), 0, 4) < 3).astype(jnp.int32), jax.random.fold_in(splits[1], 1), 0, 1),
        "source_shifts": touch_ends(jax.random.randint(splits[2], (SOURCES, 2), 0, MW - K + 1), jax.random.fold_in(splits[2], 1), 0, MW - K).astype(jnp.int32),
        "source_weights": draw_source_weights(jax.random.fold_in(splits[4], 71), 0),
    }


diffusion_rate = 0.2


def phase_table(positions, frequency_count, frame_points):
    frequency = jnp.arange(frequency_count, dtype=jnp.int32) - frequency_count // 2
    phase_turns = (positions[:, None] * frequency[None, :]) % frame_points
    phase_angle = phase_turns.astype(jnp.float32) * (2.0 * jnp.pi / frame_points)
    return jnp.cos(phase_angle), jnp.sin(phase_angle)


def rotation_table(cosine, sine):
    upper = jnp.concatenate([cosine, -sine], axis=1)
    lower = jnp.concatenate([sine, cosine], axis=1)
    return jnp.concatenate([upper, lower], axis=0).astype(jnp.bfloat16)


def diffuse(level, padded):
    beside = padded[2:, 1:-1] + padded[:-2, 1:-1] + padded[1:-1, 2:] + padded[1:-1, :-2]
    return level + diffusion_rate * (beside - 4.0 * level)


def reference(spectrum, pupil_mask, source_shifts, source_weights):
    passband = pupil_mask.shape[0]
    pupil_bf = pupil_mask.astype(jnp.bfloat16)
    row_cos, row_sin = phase_table(jnp.arange(NX, dtype=jnp.int32), passband, FRAME)
    row_table = rotation_table(row_cos, row_sin).astype(jnp.float32)
    col_cos, col_sin = phase_table(jnp.arange(NY, dtype=jnp.int32), passband, FRAME)
    col_table = jnp.concatenate([col_cos.T, col_sin.T], axis=1).astype(jnp.bfloat16).astype(jnp.float32)

    def one_source(running, item):
        shift_pair, weight_value = item
        window_cut = lax.dynamic_slice(spectrum, (jnp.int32(0), shift_pair[0].astype(jnp.int32), shift_pair[1].astype(jnp.int32)), (2, passband, passband)) * pupil_bf
        product = jnp.dot(window_cut.reshape(2 * passband, passband).astype(jnp.float32), col_table)
        real_part = product[:passband, :NY] - product[passband:, NY:]
        imag_part = product[:passband, NY:] + product[passband:, :NY]
        inner_block = jnp.concatenate([real_part, imag_part], axis=0).astype(jnp.bfloat16)
        field_pair = jnp.dot(row_table, inner_block.astype(jnp.float32))
        square = field_pair[:NX] ** 2 + field_pair[NX:] ** 2
        return running + weight_value.astype(jnp.float32) * square, None

    intensity_sum, _ = lax.scan(one_source, jnp.zeros((NX, NY), jnp.float32), (source_shifts, source_weights))
    intensity = intensity_sum / (2.0 * SOURCES)
    acid_level = 1.0 - jnp.exp(-intensity)
    for repeat in range(2):
        padded = jnp.pad(acid_level, 1)
        acid_level = diffuse(acid_level, padded)
    return acid_level
```

```python
import jax
import jax.numpy as jnp
import numpy as np
from jax import lax
from jax.experimental import pallas as pl
from jax.experimental.pallas import tpu as pltpu
from jax.sharding import Mesh
from jax.sharding import PartitionSpec as P

FRAME = 2048
PASS = 256
MASK_ROWS = 512
SOURCES = 256
ROWS = 64
COLS = 256
ROW_SPAN = 72
BATCH = 4
WEIGHT_UNIT = 1 << 18
COLUMN_UNIT = 1 << 9
DIFFUSION = 0.2


def turn_cos_sin(turns):
    shifted = turns + 256
    quadrant = (shifted >> 9) & 3
    angle = ((shifted & 511) - 256).astype(jnp.float32) * (2.0 * jnp.pi / FRAME)
    square = angle * angle
    sine = angle * (
        1.0 + square * (-1.0 / 6 + square * (1.0 / 120 + square * (-1.0 / 5040 + square * (1.0 / 362880))))
    )
    cosine = 1.0 + square * (-0.5 + square * (1.0 / 24 + square * (-1.0 / 720 + square * (1.0 / 40320))))
    odd = (quadrant & 1) == 1
    cos_part = jnp.where(odd, sine, cosine)
    sin_part = jnp.where(odd, cosine, sine)
    cos_part = jnp.where((quadrant == 1) | (quadrant == 2), -cos_part, cos_part)
    sin_part = jnp.where(quadrant >= 2, -sin_part, sin_part)
    return cos_part, sin_part


def iota(shape, dim):
    return lax.broadcasted_iota(jnp.int32, shape, dim)


def image_kernel(
    place_ref, codes_ref, own_ref, other_ref, pupil_ref, out_ref,
    spectrum, row_table, col_table, pupil, windows, lhs, total, total_edge, order,
):
    row0 = place_ref[0]
    col0 = place_ref[1]
    core = place_ref[2]

    count = jnp.int32(0)
    for s in range(SOURCES):
        code = codes_ref[s // 32, s % 32]
        order[count] = code
        count = count + (code >= WEIGHT_UNIT).astype(jnp.int32)
    for s in range(BATCH):
        order[count + s] = jnp.int32(0)

    low = iota((128, 128), 1) < 64
    for half, ref in ((core, own_ref), (1 - core, other_ref)):
        for xh in range(2):
            base = pl.multiple_of((2 * xh + half) * 128, 128)
            for y in range(4):
                left = ref[xh * 8 + y * 2, 0:128, :].astype(jnp.float32)
                right = ref[xh * 8 + y * 2 + 1, 0:128, :].astype(jnp.float32)
                real = jnp.where(low, left, pltpu.roll(right, 64, 1))
                imag = jnp.where(low, pltpu.roll(left, 64, 1), right)
                spectrum[y, pl.ds(base, 128), :] = real
                spectrum[y, pl.ds(base + MASK_ROWS, 128), :] = imag
    spectrum[4, :, :] = jnp.zeros((2 * MASK_ROWS, 128), jnp.float32)
    pupil[...] = pupil_ref[...].astype(jnp.bfloat16)

    shape = (ROW_SPAN, PASS)
    line = iota(shape, 0)
    line = row0 + jnp.where(line < 66, line, line - ROW_SPAN)
    cosine, sine = turn_cos_sin(line * (iota(shape, 1) - PASS // 2))
    row_table[:, 0:PASS] = jnp.concatenate([cosine, sine], axis=0).astype(jnp.bfloat16)
    row_table[:, PASS : 2 * PASS] = jnp.concatenate([-sine, cosine], axis=0).astype(jnp.bfloat16)
    shape = (PASS, COLS)
    cosine, sine = turn_cos_sin((col0 + iota(shape, 1)) * (iota(shape, 0) - PASS // 2))
    cosine = cosine.astype(jnp.bfloat16)
    sine = sine.astype(jnp.bfloat16)
    col_table[0:PASS, 0:COLS] = cosine
    col_table[0:PASS, COLS : 2 * COLS] = sine
    col_table[PASS : 2 * PASS, 0:COLS] = -sine
    col_table[PASS : 2 * PASS, COLS : 2 * COLS] = cosine
    shape = (PASS, 128)
    lane = iota(shape, 1)
    imag_lane = ((lane >= 4) & (lane < 64)).astype(jnp.int32)
    pixel = lane - 8 * imag_lane
    pixel = col0 + jnp.where(pixel < 64, jnp.where(pixel < 0, pixel, pixel + COLS), pixel - 128)
    cosine, sine = turn_cos_sin(pixel * (iota(shape, 0) - PASS // 2))
    upper = jnp.where(imag_lane == 1, sine, cosine)
    lower = jnp.where(imag_lane == 1, cosine, -sine)
    col_table[0:PASS, 2 * COLS :] = upper.astype(jnp.bfloat16)
    col_table[PASS : 2 * PASS, 2 * COLS :] = lower.astype(jnp.bfloat16)

    total[...] = jnp.zeros_like(total)
    total_edge[...] = jnp.zeros_like(total_edge)
    lane = iota((PASS, 128), 1)

    def batch(index, carry):
        weights = []
        pieces = []
        for u in range(BATCH):
            code = order[index * BATCH + u]
            a = code & (COLUMN_UNIT - 1)
            b = (code >> 9) & (COLUMN_UNIT - 1)
            weights.append((code >> 18).astype(jnp.float32))
            tile = b >> 7
            offset = b & 127
            keep = lane < 128 - offset
            for part in range(2):
                rolled = [
                    pltpu.roll(spectrum[tile + t, pl.ds(a + part * MASK_ROWS, PASS), :], (128 - offset) & 127, 1)
                    for t in range(3)
                ]
                for t in range(2):
                    cut = jnp.where(keep, rolled[t], rolled[t + 1]).astype(jnp.bfloat16)
                    windows[u, part * PASS : (part + 1) * PASS, t * 128 : (t + 1) * 128] = (
                        cut * pupil[:, t * 128 : (t + 1) * 128]
                    )
            pieces.append(
                jnp.dot(row_table[...], windows[u], preferred_element_type=jnp.float32)
            )
        real = jnp.concatenate([p[0:ROW_SPAN] for p in pieces], axis=0)
        imag = jnp.concatenate([p[ROW_SPAN:] for p in pieces], axis=0)
        lhs[:, 0:PASS] = real.astype(jnp.bfloat16)
        lhs[:, PASS:] = imag.astype(jnp.bfloat16)
        field = jnp.dot(lhs[...], col_table[...], preferred_element_type=jnp.float32)
        gain = None
        edge = None
        for u in range(BATCH):
            block = field[u * ROW_SPAN : (u + 1) * ROW_SPAN]
            real = block[:, 0:COLS]
            imag = block[:, COLS : 2 * COLS]
            border = block[:, 2 * COLS :]
            term = weights[u] * (real * real + imag * imag)
            edge_term = weights[u] * (border * border)
            gain = term if gain is None else gain + term
            edge = edge_term if edge is None else edge + edge_term
        total[...] += gain
        total_edge[...] += edge
        return carry

    lax.fori_loop(0, (count + BATCH - 1) // BATCH, batch, 0)

    edge = total_edge[...]
    edge = edge + pltpu.roll(edge, 120, 1)
    intensity = jnp.concatenate([total[...], edge], axis=1) * (1.0 / (2 * SOURCES))
    shape = (ROW_SPAN, COLS + 128)
    line = iota(shape, 0)
    line = row0 + jnp.where(line < 66, line, line - ROW_SPAN)
    pixel = iota(shape, 1)
    pixel = col0 + jnp.where(pixel < COLS + 64, pixel, pixel - (COLS + 128))
    inside = (line >= 0) & (line < FRAME) & (pixel >= 0) & (pixel < FRAME)
    level = jnp.where(inside, 1.0 - jnp.exp(-intensity), 0.0)
    for repeat in range(2):
        beside = (
            pltpu.roll(level, ROW_SPAN - 1, 0)
            + pltpu.roll(level, 1, 0)
            + pltpu.roll(level, COLS + 127, 1)
            + pltpu.roll(level, 1, 1)
        )
        level = jnp.where(inside, level + DIFFUSION * (beside - 4.0 * level), 0.0)
    out_ref[...] = level[0:ROWS, 0:COLS]


def image_block(place, codes, own, other, pupil_mask):
    vmem = pl.BlockSpec(memory_space=pltpu.VMEM)
    smem = pl.BlockSpec(memory_space=pltpu.SMEM)
    return pl.pallas_call(
        image_kernel,
        out_shape=jax.ShapeDtypeStruct((ROWS, COLS), jnp.float32),
        in_specs=[smem, smem, vmem, vmem, vmem],
        out_specs=vmem,
        scratch_shapes=[
            pltpu.VMEM((5, 2 * MASK_ROWS, 128), jnp.float32),
            pltpu.VMEM((2 * ROW_SPAN, 2 * PASS), jnp.bfloat16),
            pltpu.VMEM((2 * PASS, 2 * COLS + 128), jnp.bfloat16),
            pltpu.VMEM((PASS, PASS), jnp.bfloat16),
            pltpu.VMEM((BATCH, 2 * PASS, PASS), jnp.bfloat16),
            pltpu.VMEM((BATCH * ROW_SPAN, 2 * PASS), jnp.bfloat16),
            pltpu.VMEM((ROW_SPAN, COLS), jnp.float32),
            pltpu.VMEM((ROW_SPAN, 128), jnp.float32),
            pltpu.SMEM((SOURCES + 2 * BATCH,), jnp.int32),
        ],
        compiler_params=pltpu.CompilerParams(vmem_limit_bytes=32 << 20),
    )(place, codes, own, other, pupil_mask)


def gather_blocks(block, axes, count):
    copies = jnp.broadcast_to(block[None], (count,) + block.shape)
    return lax.all_to_all(copies, axes, 0, 0, tiled=True)


def body(spectrum, pupil_mask, source_shifts, source_weights):
    block = jnp.concatenate([spectrum[0], spectrum[1]], axis=1)
    column = gather_blocks(block, ("z",), 8).reshape(128, 128)
    numbers = jnp.concatenate([source_shifts.T, source_weights[None]], axis=0)
    numbers = jnp.pad(numbers, ((0, 5), (0, 96))).astype(jnp.bfloat16)
    own = gather_blocks(jnp.concatenate([column, numbers], axis=0), ("xh", "y", "xl"), 16)
    other = lax.ppermute(own, "core", [(0, 1), (1, 0)])
    listed = own[0:8, 128:136, 0:32].astype(jnp.int32)
    codes = listed[:, 0] + COLUMN_UNIT * listed[:, 1] + WEIGHT_UNIT * listed[:, 2]
    core = lax.axis_index("core")
    tile = 2 * lax.axis_index("xh") + core
    group = 2 * lax.axis_index("y") + lax.axis_index("xl")
    place = jnp.stack([tile * 512 + group * ROWS, lax.axis_index("z") * COLS, core])
    return image_block(place, codes, own, other, pupil_mask)


def solution(mesh):
    fine = Mesh(np.asarray(mesh.devices).reshape(2, 2, 8, 4, 2), ("xh", "core", "z", "y", "xl"))
    tx, ty, src = ("xh", "core"), "z", ("y", "xl")
    placed = (P(None, (*tx, ty), src), P(), P(src, None), P(src))
    return jax.shard_map(
        body, mesh=fine, in_specs=placed, out_specs=P((*tx, *src), ty), check_vma=False
    )
```

```python
import jax
import jax.numpy as jnp
import numpy as np
from jax import lax
from jax.experimental import pallas as pl
from jax.experimental.pallas import tpu as pltpu
from jax.sharding import Mesh
from jax.sharding import PartitionSpec as P

FRAME = 2048
TURN = 2 * FRAME
PASS = 256
MASK_ROWS = 512
SOURCES = 256
ROWS = 64
COLS = 256
SPAN = 72
BATCH = 4
WEIGHT_UNIT = 1 << 18
COLUMN_UNIT = 1 << 9
DIFFUSION = 0.2


def turn_cos_sin(turns):
    shifted = turns + TURN // 8
    quadrant = (shifted >> 10) & 3
    angle = ((shifted & 1023) - TURN // 8).astype(jnp.float32) * (2.0 * jnp.pi / TURN)
    square = angle * angle
    sine = angle * (
        1.0 + square * (-1.0 / 6 + square * (1.0 / 120 + square * (-1.0 / 5040 + square * (1.0 / 362880))))
    )
    cosine = 1.0 + square * (-0.5 + square * (1.0 / 24 + square * (-1.0 / 720 + square * (1.0 / 40320))))
    odd = (quadrant & 1) == 1
    cos_part = jnp.where(odd, sine, cosine)
    sin_part = jnp.where(odd, cosine, sine)
    cos_part = jnp.where((quadrant == 1) | (quadrant == 2), -cos_part, cos_part)
    sin_part = jnp.where(quadrant >= 2, -sin_part, sin_part)
    return cos_part, sin_part


def iota(shape, dim):
    return lax.broadcasted_iota(jnp.int32, shape, dim)


def tables_kernel(place_ref, pupil_ref, row_table, col_table, pupil, phase_cos, phase_sin):
    pupil[...] = pupil_ref[...].astype(jnp.bfloat16)

    shape = (SPAN, PASS)
    line = iota(shape, 0)
    is_sin = ((line >= 32) & (line < 64)) | (line >= 68)
    pair = jnp.where(line < 64, line & 31, 32 + (line & 3))
    cosine, sine = turn_cos_sin((2 * pair + 1) * (iota(shape, 1) - PASS // 2))
    row_table[...] = jnp.where(is_sin, sine, cosine).astype(jnp.bfloat16)

    shape = (PASS, 128)
    frequency = iota(shape, 0) - PASS // 2
    lane = iota(shape, 1)
    cosine, sine = turn_cos_sin((2 * lane + 1) * frequency)
    col_table[:, 0:128] = cosine.astype(jnp.bfloat16)
    col_table[:, 128:256] = sine.astype(jnp.bfloat16)
    cosine, sine = turn_cos_sin((2 * (128 + (lane & 1)) + 1) * frequency)
    col_table[:, 256:384] = cosine.astype(jnp.bfloat16)
    col_table[:, 384:512] = jnp.where((lane & 2) == 0, sine, -sine).astype(jnp.bfloat16)

    row_turns = 2 * place_ref[0] + ROWS - 1
    col_turns = 2 * place_ref[1] + COLS - 1
    shape = (MASK_ROWS, 128)
    row_cos, row_sin = turn_cos_sin(row_turns * iota(shape, 0))
    for tile in range(4):
        col_cos, col_sin = turn_cos_sin(col_turns * (iota((8, 128), 1) + 128 * tile))
        col_cos, col_sin = col_cos[0:1], col_sin[0:1]
        phase_cos[tile] = row_cos * col_cos - row_sin * col_sin
        phase_sin[tile] = row_sin * col_cos + row_cos * col_sin


def image_kernel(
    place_ref, codes_ref, own_ref, other_ref, row_table, col_table, pupil, phase_cos, phase_sin, out_ref,
    spectrum, lhs_even, lhs_odd, plus, minus, edges, order,
):
    row0 = place_ref[0]
    col0 = place_ref[1]
    core = place_ref[2]

    count = jnp.int32(0)
    for s in range(SOURCES):
        code = codes_ref[s // 32, s % 32]
        order[count] = code
        count = count + (code >= WEIGHT_UNIT).astype(jnp.int32)
    for s in range(3 * BATCH):
        order[count + s] = jnp.int32(0)

    low = iota((128, 128), 1) < 64
    for half, ref in ((core, own_ref), (1 - core, other_ref)):
        for xh in range(2):
            base = pl.multiple_of((2 * xh + half) * 128, 128)
            for y in range(4):
                left = ref[xh * 8 + y * 2, 0:128, :].astype(jnp.float32)
                right = ref[xh * 8 + y * 2 + 1, 0:128, :].astype(jnp.float32)
                real = jnp.where(low, left, pltpu.roll(right, 64, 1))
                imag = jnp.where(low, pltpu.roll(left, 64, 1), right)
                cosine = phase_cos[y, pl.ds(base, 128), :]
                sine = phase_sin[y, pl.ds(base, 128), :]
                spectrum[y, pl.ds(base, 128), :] = real * cosine - imag * sine
                spectrum[y, pl.ds(base + MASK_ROWS, 128), :] = real * sine + imag * cosine
    spectrum[4, :, :] = jnp.zeros((2 * MASK_ROWS, 128), jnp.float32)

    plus[...] = jnp.zeros_like(plus)
    minus[...] = jnp.zeros_like(minus)
    edges[...] = jnp.zeros_like(edges)
    lane = iota((PASS, 128), 1)
    fold_lane = iota((SPAN, 128), 1)
    upper = iota((8, 128), 0) < 4
    blank = jnp.zeros((PASS, 128), jnp.bfloat16)

    def row_transform(index, lhs):
        steps = [(u, t) for u in range(BATCH) for t in range(3)]
        codes = [order[index * BATCH + u] for u in range(BATCH)]
        kept = {}

        def prepare(u, t):
            a = codes[u] & (COLUMN_UNIT - 1)
            b = (codes[u] >> 9) & (COLUMN_UNIT - 1)
            offset = b & 127
            moved = pltpu.roll(pupil[:, t * 128 : (t + 1) * 128], offset, 1) if t < 2 else blank
            before = (iota((16, 128), 1) < offset).astype(jnp.bfloat16)
            mask = (moved.reshape(16,16,128) + before * (kept.get(u, blank).reshape(16, 16, 128) - moved.reshape(16, 16, 128))).reshape(PASS, 128)
            kept[u] = moved
            return jnp.concatenate(
                [
                    spectrum[(b >> 7) + t, pl.ds(a + part * MASK_ROWS, PASS), :].astype(jnp.bfloat16) * mask
                    for part in range(2)
                ],
                axis=1,
            )

        last_re, last_im = None, None
        window = prepare(*steps[0])
        for n, (u, t) in enumerate(steps):
            pair = jnp.dot(row_table[...], window, preferred_element_type=jnp.float32)
            if n + 1 < len(steps):
                window = prepare(*steps[n + 1])
            offset = (codes[u] >> 9) & 127
            back = (128 - offset) & 127
            real, imag = pair[:, 0:128], pair[:, 128:256]
            cos_re, sin_re, mix_re = real[0:32], real[32:64], real[64:72]
            cos_im, sin_im, mix_im = imag[0:32], imag[32:64], imag[64:72]
            swap_re, swap_im = pltpu.roll(mix_re, 4, 0), pltpu.roll(mix_im, 4, 0)
            real = jnp.concatenate(
                [cos_re - sin_im, cos_re + sin_im, jnp.where(upper, mix_re - swap_im, swap_re + mix_im)], axis=0
            )
            imag = jnp.concatenate(
                [cos_im + sin_re, cos_im - sin_re, jnp.where(upper, mix_im + swap_re, swap_im - mix_re)], axis=0
            )
            real, imag = pltpu.roll(real, back, 1), pltpu.roll(imag, back, 1)
            if t > 0:
                keep = fold_lane < 128 - offset
                full_re, full_im = jnp.where(keep, last_re, real), jnp.where(keep, last_im, imag)
                rows = []
                for g in range(SPAN // 8):
                    rows += [full_re[8 * g : 8 * g + 8], full_im[8 * g : 8 * g + 8]]
                lhs[u * 2 * SPAN : (u + 1) * 2 * SPAN, (t - 1) * 128 : t * 128] = jnp.concatenate(
                    rows, axis=0
                ).astype(jnp.bfloat16)
            last_re, last_im = real, imag

    def column_transform(index, lhs):
        field = jnp.dot(lhs[...], col_table[...], preferred_element_type=jnp.float32)
        weights = [(order[index * BATCH + u] >> 18).astype(jnp.float32) for u in range(BATCH)]
        for g in range(SPAN // 8):
            here = slice(8 * g, 8 * g + 8)
            sums = [plus[here, :], minus[here, :], edges[here, :]]
            for u in range(BATCH):
                first = u * 2 * SPAN + 16 * g
                real, imag = field[first : first + 8], field[first + 8 : first + 16]
                cos_re, sin_re, cos_im, sin_im = real[:, 0:128], real[:, 128:256], imag[:, 0:128], imag[:, 128:256]
                right_re, right_im = cos_re - sin_im, cos_im + sin_re
                left_re, left_im = cos_re + sin_im, cos_im - sin_re
                edge_re, edge_im = real[:, 256:384] - imag[:, 384:512], imag[:, 256:384] + real[:, 384:512]
                sums[0] = sums[0] + weights[u] * (right_re * right_re + right_im * right_im)
                sums[1] = sums[1] + weights[u] * (left_re * left_re + left_im * left_im)
                sums[2] = sums[2] + weights[u] * (edge_re * edge_re + edge_im * edge_im)
            plus[here, :], minus[here, :], edges[here, :] = sums

    row_transform(0, lhs_even)

    def two_batches(index, carry):
        column_transform(2 * index, lhs_even)
        row_transform(2 * index + 1, lhs_odd)
        column_transform(2 * index + 1, lhs_odd)
        row_transform(2 * index + 2, lhs_even)
        return carry

    lax.fori_loop(0, (count + 2 * BATCH - 1) // (2 * BATCH), two_batches, 0)

    def place_by(left, right):
        return jnp.dot(left, right, precision=lax.Precision.HIGHEST, preferred_element_type=jnp.float32)

    source, target = iota((128, 128), 0), iota((128, 128), 1)
    mirror = (source + target == 127).astype(jnp.float32)
    beyond = ((source == target) & (source < 2)) | ((source + target == 129) & (source >= 2) & (source < 4))
    folded = jnp.concatenate(
        [place_by(minus[...], mirror), plus[...], place_by(edges[...], beyond.astype(jnp.float32))], axis=1
    )
    target, source = iota((SPAN, SPAN), 0), iota((SPAN, SPAN), 1)
    wanted = jnp.where(
        target < 32, 63 - target, jnp.where(target < 64, target - 32, jnp.where(target < 68, target, 139 - target))
    )
    intensity = place_by((source == wanted).astype(jnp.float32), folded) * (1.0 / (2 * SOURCES))

    shape = (SPAN, COLS + 128)
    line = iota(shape, 0)
    line = row0 + jnp.where(line < 66, line, line - SPAN)
    pixel = iota(shape, 1)
    pixel = col0 + jnp.where(pixel < COLS + 64, pixel, pixel - (COLS + 128))
    inside = (line >= 0) & (line < FRAME) & (pixel >= 0) & (pixel < FRAME)
    level = jnp.where(inside, 1.0 - jnp.exp(-intensity), 0.0)
    for repeat in range(2):
        beside = (
            pltpu.roll(level, SPAN - 1, 0)
            + pltpu.roll(level, 1, 0)
            + pltpu.roll(level, COLS + 127, 1)
            + pltpu.roll(level, 1, 1)
        )
        level = jnp.where(inside, level + DIFFUSION * (beside - 4.0 * level), 0.0)
    out_ref[...] = level[0:ROWS, 0:COLS]


VMEM_SPEC = pl.BlockSpec(memory_space=pltpu.VMEM)
SMEM_SPEC = pl.BlockSpec(memory_space=pltpu.SMEM)


def make_tables(place, pupil_mask):
    return pl.pallas_call(
        tables_kernel,
        out_shape=(
            jax.ShapeDtypeStruct((SPAN, PASS), jnp.bfloat16),
            jax.ShapeDtypeStruct((PASS, 512), jnp.bfloat16),
            jax.ShapeDtypeStruct((PASS, PASS), jnp.bfloat16),
            jax.ShapeDtypeStruct((4, MASK_ROWS, 128), jnp.float32),
            jax.ShapeDtypeStruct((4, MASK_ROWS, 128), jnp.float32),
        ),
        in_specs=[SMEM_SPEC, VMEM_SPEC],
        out_specs=(VMEM_SPEC,) * 5,
        compiler_params=pltpu.CompilerParams(vmem_limit_bytes=16 << 20),
        cost_estimate=pl.CostEstimate(flops=8_000_000, bytes_accessed=3_000_000, transcendentals=0),
    )(place, pupil_mask)


def image_block(place, codes, own, other, tables):
    return pl.pallas_call(
        image_kernel,
        out_shape=jax.ShapeDtypeStruct((ROWS, COLS), jnp.float32),
        in_specs=[SMEM_SPEC, SMEM_SPEC] + [VMEM_SPEC] * 7,
        out_specs=VMEM_SPEC,
        scratch_shapes=[
            pltpu.VMEM((5, 2 * MASK_ROWS, 128), jnp.float32),
            pltpu.VMEM((BATCH * 2 * SPAN, PASS), jnp.bfloat16),
            pltpu.VMEM((BATCH * 2 * SPAN, PASS), jnp.bfloat16),
            pltpu.VMEM((SPAN, 128), jnp.float32),
            pltpu.VMEM((SPAN, 128), jnp.float32),
            pltpu.VMEM((SPAN, 128), jnp.float32),
            pltpu.SMEM((SOURCES + 4 * BATCH,), jnp.int32),
        ],
        compiler_params=pltpu.CompilerParams(vmem_limit_bytes=32 << 20),
    )(place, codes, own, other, *tables)


def gather_blocks(block, axes, count):
    copies = jnp.broadcast_to(block[None], (count,) + block.shape)
    return lax.all_to_all(copies, axes, 0, 0, tiled=True)


def body(spectrum, pupil_mask, source_shifts, source_weights):
    block = jnp.concatenate([spectrum[0], spectrum[1]], axis=1)
    column = gather_blocks(block, ("z",), 8).reshape(128, 128)
    numbers = jnp.concatenate([source_shifts.T, source_weights[None]], axis=0)
    numbers = jnp.pad(numbers, ((0, 5), (0, 96))).astype(jnp.bfloat16)
    own = gather_blocks(jnp.concatenate([column, numbers], axis=0), ("xh", "y", "xl"), 16)
    other = lax.ppermute(own, "core", [(0, 1), (1, 0)])
    listed = own[0:8, 128:136, 0:32].astype(jnp.int32)
    codes = listed[:, 0] + COLUMN_UNIT * listed[:, 1] + WEIGHT_UNIT * listed[:, 2]
    core = lax.axis_index("core")
    tile = 2 * lax.axis_index("xh") + core
    group = 2 * lax.axis_index("y") + lax.axis_index("xl")
    place = jnp.stack([tile * 512 + group * ROWS, lax.axis_index("z") * COLS, core])
    return image_block(place, codes, own, other, make_tables(place, pupil_mask))


def solution(mesh):
    fine = Mesh(np.asarray(mesh.devices).reshape(2, 2, 8, 4, 2), ("xh", "core", "z", "y", "xl"))
    tx, ty, src = ("xh", "core"), "z", ("y", "xl")
    placed = (P(None, (*tx, ty), src), P(), P(src, None), P(src))
    return jax.shard_map(
        body, mesh=fine, in_specs=placed, out_specs=P((*tx, *src), ty), check_vma=False
    )
```

```python
import jax
import jax.numpy as jnp
import numpy as np
from jax import lax
from jax.experimental import pallas as pl
from jax.experimental.pallas import tpu as pltpu
from jax.sharding import Mesh
from jax.sharding import PartitionSpec as P

FRAME = 2048
TURN = 2 * FRAME
PASS = 256
MASK_ROWS = 512
SOURCES = 256
ROWS = 64
COLS = 256
SPAN = 72
TABLE_ROWS = 80
BATCH = 4
TOP_WEIGHT = 8
WEIGHT_UNIT = 1 << 18
COLUMN_UNIT = 1 << 9
DIFFUSION = 0.2


def turn_cos_sin(turns):
    shifted = turns + TURN // 8
    quadrant = (shifted >> 10) & 3
    angle = ((shifted & 1023) - TURN // 8).astype(jnp.float32) * (2.0 * jnp.pi / TURN)
    square = angle * angle
    sine = angle * (
        1.0 + square * (-1.0 / 6 + square * (1.0 / 120 + square * (-1.0 / 5040 + square * (1.0 / 362880))))
    )
    cosine = 1.0 + square * (-0.5 + square * (1.0 / 24 + square * (-1.0 / 720 + square * (1.0 / 40320))))
    odd = (quadrant & 1) == 1
    cos_part = jnp.where(odd, sine, cosine)
    sin_part = jnp.where(odd, cosine, sine)
    cos_part = jnp.where((quadrant == 1) | (quadrant == 2), -cos_part, cos_part)
    sin_part = jnp.where(quadrant >= 2, -sin_part, sin_part)
    return cos_part, sin_part


def iota(shape, dim):
    return lax.broadcasted_iota(jnp.int32, shape, dim)


def tables_kernel(place_ref, pupil_ref, row_table, col_table, pupil, phase_cos, phase_sin):
    whole = pupil_ref[...].astype(jnp.float32)
    for part, half in enumerate((whole[:, 0:128], whole[:, 128:256], whole[:, 0:128] - whole[:, 128:256])):
        pupil[part] = half.astype(jnp.bfloat16)

    shape = (TABLE_ROWS, PASS)
    line = iota(shape, 0)
    is_sin = ((line >= 32) & (line < 64)) | (line >= 72)
    pair = jnp.where(line < 64, line & 31, 32 + (line & 1))
    cosine, sine = turn_cos_sin((2 * pair + 1) * (iota(shape, 1) - PASS // 2))
    wave = jnp.where(is_sin, jnp.where((line >= 64) & ((line & 2) == 2), -sine, sine), cosine)
    for weight in range(TOP_WEIGHT + 1):
        row_table[weight] = (weight**0.5 * wave).astype(jnp.bfloat16)

    shape = (PASS, 128)
    frequency = iota(shape, 0) - PASS // 2
    lane = iota(shape, 1)
    cosine, sine = turn_cos_sin((2 * lane + 1) * frequency)
    col_table[:, 0:128] = cosine.astype(jnp.bfloat16)
    col_table[:, 128:256] = sine.astype(jnp.bfloat16)
    cosine, sine = turn_cos_sin((2 * (128 + (lane & 1)) + 1) * frequency)
    col_table[:, 256:384] = cosine.astype(jnp.bfloat16)
    col_table[:, 384:512] = jnp.where((lane & 2) == 0, sine, -sine).astype(jnp.bfloat16)

    row_turns = 2 * place_ref[0] + ROWS - 1
    col_turns = 2 * place_ref[1] + COLS - 1
    shape = (MASK_ROWS, 128)
    row_cos, row_sin = turn_cos_sin(row_turns * iota(shape, 0))
    for tile in range(4):
        col_cos, col_sin = turn_cos_sin(col_turns * (iota((8, 128), 1) + 128 * tile))
        col_cos, col_sin = col_cos[0:1], col_sin[0:1]
        phase_cos[tile] = row_cos * col_cos - row_sin * col_sin
        phase_sin[tile] = row_sin * col_cos + row_cos * col_sin


def image_kernel(
    place_ref, codes_ref, own_ref, other_ref, row_table, col_table, pupil, phase_cos, phase_sin, out_ref,
    spectrum, lhs_even, lhs_odd, plus, minus, edges, order,
):
    row0 = place_ref[0]
    col0 = place_ref[1]
    core = place_ref[2]

    count = jnp.int32(0)
    for s in range(SOURCES):
        code = codes_ref[s // 32, s % 32]
        order[count] = code
        count = count + (code >= WEIGHT_UNIT).astype(jnp.int32)
    for s in range(3 * BATCH):
        order[count + s] = jnp.int32(0)

    low = iota((128, 128), 1) < 64
    for half, ref in ((core, own_ref), (1 - core, other_ref)):
        for xh in range(2):
            base = pl.multiple_of((2 * xh + half) * 128, 128)
            for y in range(4):
                left = ref[xh * 8 + y * 2, 0:128, :].astype(jnp.float32)
                right = ref[xh * 8 + y * 2 + 1, 0:128, :].astype(jnp.float32)
                real = jnp.where(low, left, pltpu.roll(right, 64, 1))
                imag = jnp.where(low, pltpu.roll(left, 64, 1), right)
                cosine = phase_cos[y, pl.ds(base, 128), :]
                sine = phase_sin[y, pl.ds(base, 128), :]
                spectrum[y, pl.ds(base, 128), :] = real * cosine - imag * sine
                spectrum[y, pl.ds(base + MASK_ROWS, 128), :] = real * sine + imag * cosine
    spectrum[4, :, :] = jnp.zeros((2 * MASK_ROWS, 128), jnp.float32)

    plus[...] = jnp.zeros_like(plus)
    minus[...] = jnp.zeros_like(minus)
    edges[...] = jnp.zeros_like(edges)
    sublane_lane = iota((16, 128), 1)
    lane = iota((PASS, 128), 1)
    fold_lane = iota((2 * SPAN, 128), 1)

    def row_transform(index, lhs, members=range(BATCH)):
        for u in members:
            code = order[index * BATCH + u]
            a = code & (COLUMN_UNIT - 1)
            b = (code >> 9) & (COLUMN_UNIT - 1)
            tile = b >> 7
            offset = b & 127
            back = (128 - offset) & 127
            before = (sublane_lane < offset).astype(jnp.bfloat16)
            left, right = [pltpu.roll(pupil[h], offset, 1).reshape(16, 16, 128) for h in range(2)]
            change = before * (left - right)
            masks = [(left - change).reshape(PASS, 128), (right + change).reshape(PASS, 128)]
            turned = []
            for t in range(2):
                window = []
                for part in range(2):
                    rows = pl.ds(a + part * MASK_ROWS, PASS)
                    piece = spectrum[tile + t, rows, :]
                    if t == 0:
                        piece = jnp.where(lane < offset, spectrum[tile + 2, rows, :], piece)
                    window.append(piece.astype(jnp.bfloat16) * masks[t])
                pair = jnp.dot(row_table[code >> 18], jnp.concatenate(window, axis=1), preferred_element_type=jnp.float32)
                rows = []
                for g in range(SPAN // 8):
                    first, second = (8 * (g & 3), 32 + 8 * (g & 3)) if g < 8 else (64, 72)
                    cos_re, sin_re = pair[first : first + 8, 0:128], pair[second : second + 8, 0:128]
                    cos_im, sin_im = pair[first : first + 8, 128:256], pair[second : second + 8, 128:256]
                    rows += [cos_re + sin_im, cos_im - sin_re] if 4 <= g < 8 else [cos_re - sin_im, cos_im + sin_re]
                turned.append(jnp.concatenate(rows, axis=0))
            inside = fold_lane >= offset
            for t in range(2):
                lhs[u * 2 * SPAN : (u + 1) * 2 * SPAN, t * 128 : (t + 1) * 128] = pltpu.roll(
                    jnp.where(inside, turned[t], turned[1 - t]).astype(jnp.bfloat16), back, 1
                )

    def column_transform(index, lhs, members=range(BATCH)):
        span = slice(members[0] * 2 * SPAN, (members[-1] + 1) * 2 * SPAN)
        field = jnp.dot(lhs[span, :], col_table[...], preferred_element_type=jnp.float32)
        for g in range(SPAN // 8):
            here = slice(8 * g, 8 * g + 8)
            sums = [plus[here, :], minus[here, :], edges[here, :]]
            for u in range(len(members)):
                first = u * 2 * SPAN + 16 * g
                real, imag = field[first : first + 8], field[first + 8 : first + 16]
                cos_re, sin_re, cos_im, sin_im = real[:, 0:128], real[:, 128:256], imag[:, 0:128], imag[:, 128:256]
                right_re, right_im = cos_re - sin_im, cos_im + sin_re
                left_re, left_im = cos_re + sin_im, cos_im - sin_re
                edge_re, edge_im = real[:, 256:384] - imag[:, 384:512], imag[:, 256:384] + real[:, 384:512]
                sums[0] = sums[0] + (right_re * right_re + right_im * right_im)
                sums[1] = sums[1] + (left_re * left_re + left_im * left_im)
                sums[2] = sums[2] + (edge_re * edge_re + edge_im * edge_im)
            plus[here, :], minus[here, :], edges[here, :] = sums

    row_transform(0, lhs_even)

    def two_batches(index, carry):
        half = BATCH // 2
        for old, new, step in ((lhs_even, lhs_odd, 0), (lhs_odd, lhs_even, 1)):
            for part in (range(half), range(half, BATCH)):
                column_transform(2 * index + step, old, part)
                row_transform(2 * index + step + 1, new, part)
        return carry

    batches = jnp.maximum((count + BATCH - 1) // BATCH, 1)
    whole = (batches - 1) // 2
    lax.fori_loop(0, whole, two_batches, 0)
    column_transform(2 * whole, lhs_even)

    @pl.when(2 * whole + 1 < batches)
    def last_batch():
        row_transform(2 * whole + 1, lhs_odd)
        column_transform(2 * whole + 1, lhs_odd)

    def place_by(left, right):
        return jnp.dot(left, right, precision=lax.Precision.HIGHEST, preferred_element_type=jnp.float32)

    source, target = iota((128, 128), 0), iota((128, 128), 1)
    mirror = (source + target == 127).astype(jnp.float32)
    beyond = ((source == target) & (source < 2)) | ((source + target == 129) & (source >= 2) & (source < 4))
    folded = jnp.concatenate(
        [place_by(minus[...], mirror), plus[...], place_by(edges[...], beyond.astype(jnp.float32))], axis=1
    )
    target, source = iota((SPAN, SPAN), 0), iota((SPAN, SPAN), 1)
    wanted = jnp.where(
        target < 32, 63 - target, jnp.where(target < 64, target - 32, jnp.where(target < 68, target, 137 - target))
    )
    intensity = place_by((source == wanted).astype(jnp.float32), folded) * (1.0 / (2 * SOURCES))

    shape = (SPAN, COLS + 128)
    line = iota(shape, 0)
    line = row0 + jnp.where(line < 66, line, line - SPAN)
    pixel = iota(shape, 1)
    pixel = col0 + jnp.where(pixel < COLS + 64, pixel, pixel - (COLS + 128))
    inside = (line >= 0) & (line < FRAME) & (pixel >= 0) & (pixel < FRAME)
    level = jnp.where(inside, 1.0 - jnp.exp(-intensity), 0.0)
    for repeat in range(2):
        beside = (
            pltpu.roll(level, SPAN - 1, 0)
            + pltpu.roll(level, 1, 0)
            + pltpu.roll(level, COLS + 127, 1)
            + pltpu.roll(level, 1, 1)
        )
        level = jnp.where(inside, level + DIFFUSION * (beside - 4.0 * level), 0.0)
    out_ref[...] = level[0:ROWS, 0:COLS]


VMEM_SPEC = pl.BlockSpec(memory_space=pltpu.VMEM)
SMEM_SPEC = pl.BlockSpec(memory_space=pltpu.SMEM)


def make_tables(place, pupil_mask):
    return pl.pallas_call(
        tables_kernel,
        out_shape=(
            jax.ShapeDtypeStruct((TOP_WEIGHT + 1, TABLE_ROWS, PASS), jnp.bfloat16),
            jax.ShapeDtypeStruct((PASS, 512), jnp.bfloat16),
            jax.ShapeDtypeStruct((3, PASS, 128), jnp.bfloat16),
            jax.ShapeDtypeStruct((4, MASK_ROWS, 128), jnp.float32),
            jax.ShapeDtypeStruct((4, MASK_ROWS, 128), jnp.float32),
        ),
        in_specs=[SMEM_SPEC, VMEM_SPEC],
        out_specs=(VMEM_SPEC,) * 5,
        compiler_params=pltpu.CompilerParams(vmem_limit_bytes=16 << 20),
        cost_estimate=pl.CostEstimate(flops=8_000_000, bytes_accessed=3_000_000, transcendentals=0),
    )(place, pupil_mask)


def image_block(place, codes, own, other, tables):
    return pl.pallas_call(
        image_kernel,
        out_shape=jax.ShapeDtypeStruct((ROWS, COLS), jnp.float32),
        in_specs=[SMEM_SPEC, SMEM_SPEC] + [VMEM_SPEC] * 7,
        out_specs=VMEM_SPEC,
        scratch_shapes=[
            pltpu.VMEM((5, 2 * MASK_ROWS, 128), jnp.float32),
            pltpu.VMEM((BATCH * 2 * SPAN, PASS), jnp.bfloat16),
            pltpu.VMEM((BATCH * 2 * SPAN, PASS), jnp.bfloat16),
            pltpu.VMEM((SPAN, 128), jnp.float32),
            pltpu.VMEM((SPAN, 128), jnp.float32),
            pltpu.VMEM((SPAN, 128), jnp.float32),
            pltpu.SMEM((SOURCES + 4 * BATCH,), jnp.int32),
        ],
        compiler_params=pltpu.CompilerParams(vmem_limit_bytes=32 << 20),
    )(place, codes, own, other, *tables)


def gather_blocks(block, axes, count):
    copies = jnp.broadcast_to(block[None], (count,) + block.shape)
    return lax.all_to_all(copies, axes, 0, 0, tiled=True)


def body(spectrum, pupil_mask, source_shifts, source_weights):
    block = jnp.concatenate([spectrum[0], spectrum[1]], axis=1)
    column = gather_blocks(block, ("z",), 8).reshape(128, 128)
    numbers = jnp.concatenate([source_shifts.T, source_weights[None]], axis=0)
    numbers = jnp.pad(numbers, ((0, 5), (0, 96))).astype(jnp.bfloat16)
    own = gather_blocks(jnp.concatenate([column, numbers], axis=0), ("xh", "y", "xl"), 16)
    other = lax.ppermute(own, "core", [(0, 1), (1, 0)])
    listed = own[0:8, 128:136, 0:32].astype(jnp.int32)
    codes = listed[:, 0] + COLUMN_UNIT * listed[:, 1] + WEIGHT_UNIT * listed[:, 2]
    core = lax.axis_index("core")
    tile = 2 * lax.axis_index("xh") + core
    group = 2 * lax.axis_index("y") + lax.axis_index("xl")
    place = jnp.stack([tile * 512 + group * ROWS, lax.axis_index("z") * COLS, core])
    return image_block(place, codes, own, other, make_tables(place, pupil_mask))


def solution(mesh):
    fine = Mesh(np.asarray(mesh.devices).reshape(2, 2, 8, 4, 2), ("xh", "core", "z", "y", "xl"))
    tx, ty, src = ("xh", "core"), "z", ("y", "xl")
    placed = (P(None, (*tx, ty), src), P(), P(src, None), P(src))
    return jax.shard_map(
        body, mesh=fine, in_specs=placed, out_specs=P((*tx, *src), ty), check_vma=False
    )
```

```python
import jax
import jax.numpy as jnp
import numpy as np
from jax import lax
from jax.experimental import pallas as pl
from jax.experimental.pallas import tpu as pltpu
from jax.sharding import Mesh
from jax.sharding import PartitionSpec as P

FRAME = 2048
TURN = 2 * FRAME
PASS = 256
MASK_ROWS = 512
SOURCES = 256
ROWS = 64
COLS = 256
SPAN = 72
TABLE_ROWS = 80
BATCH = 4
TOP_WEIGHT = 8
WEIGHT_UNIT = 1 << 18
COLUMN_UNIT = 1 << 9
DIFFUSION = 0.2


def turn_cos_sin(turns):
    shifted = turns + TURN // 8
    quadrant = (shifted >> 10) & 3
    angle = ((shifted & 1023) - TURN // 8).astype(jnp.float32) * (2.0 * jnp.pi / TURN)
    square = angle * angle
    sine = angle * (
        1.0 + square * (-1.0 / 6 + square * (1.0 / 120 + square * (-1.0 / 5040 + square * (1.0 / 362880))))
    )
    cosine = 1.0 + square * (-0.5 + square * (1.0 / 24 + square * (-1.0 / 720 + square * (1.0 / 40320))))
    odd = (quadrant & 1) == 1
    cos_part = jnp.where(odd, sine, cosine)
    sin_part = jnp.where(odd, cosine, sine)
    cos_part = jnp.where((quadrant == 1) | (quadrant == 2), -cos_part, cos_part)
    sin_part = jnp.where(quadrant >= 2, -sin_part, sin_part)
    return cos_part, sin_part


def iota(shape, dim):
    return lax.broadcasted_iota(jnp.int32, shape, dim)


def tables_kernel(place_ref, pupil_ref, row_table, col_table, pupil, phase_cos, phase_sin):
    whole = pupil_ref[...].astype(jnp.float32)
    for part, half in enumerate((whole[:, 0:128], whole[:, 128:256], whole[:, 0:128] - whole[:, 128:256])):
        pupil[part] = half.astype(jnp.bfloat16)

    shape = (TABLE_ROWS, PASS)
    line = iota(shape, 0)
    is_sin = ((line >= 32) & (line < 64)) | (line >= 72)
    pair = jnp.where(line < 64, line & 31, 32 + (line & 1))
    cosine, sine = turn_cos_sin((2 * pair + 1) * (iota(shape, 1) - PASS // 2))
    wave = jnp.where(is_sin, jnp.where((line >= 64) & ((line & 2) == 2), -sine, sine), cosine)
    for weight in range(TOP_WEIGHT + 1):
        row_table[weight] = (weight**0.5 * wave).astype(jnp.bfloat16)

    shape = (PASS, 128)
    frequency = iota(shape, 0) - PASS // 2
    lane = iota(shape, 1)
    cosine, sine = turn_cos_sin((2 * lane + 1) * frequency)
    col_table[:, 0:128] = cosine.astype(jnp.bfloat16)
    col_table[:, 128:256] = sine.astype(jnp.bfloat16)
    cosine, sine = turn_cos_sin((2 * (128 + (lane & 1)) + 1) * frequency)
    col_table[:, 256:384] = cosine.astype(jnp.bfloat16)
    col_table[:, 384:512] = jnp.where((lane & 2) == 0, sine, -sine).astype(jnp.bfloat16)

    row_turns = 2 * place_ref[0] + ROWS - 1
    col_turns = 2 * place_ref[1] + COLS - 1
    shape = (MASK_ROWS, 128)
    row_cos, row_sin = turn_cos_sin(row_turns * iota(shape, 0))
    for tile in range(4):
        col_cos, col_sin = turn_cos_sin(col_turns * (iota((8, 128), 1) + 128 * tile))
        col_cos, col_sin = col_cos[0:1], col_sin[0:1]
        phase_cos[tile] = row_cos * col_cos - row_sin * col_sin
        phase_sin[tile] = row_sin * col_cos + row_cos * col_sin


def image_kernel(
    place_ref, codes_ref, own_ref, other_ref, row_table, col_table, pupil, phase_cos, phase_sin, out_ref,
    spectrum, lhs_even, lhs_odd, plus, minus, edges, order,
):
    row0 = place_ref[0]
    col0 = place_ref[1]
    core = place_ref[2]

    count = jnp.int32(0)
    for s in range(SOURCES):
        code = codes_ref[s // 32, s % 32]
        order[count] = code
        count = count + (code >= WEIGHT_UNIT).astype(jnp.int32)
    for s in range(3 * BATCH):
        order[count + s] = jnp.int32(0)

    low = iota((128, 128), 1) < 64
    for half, ref in ((core, own_ref), (1 - core, other_ref)):
        for xh in range(2):
            base = pl.multiple_of((2 * xh + half) * 128, 128)
            for y in range(4):
                left = ref[xh * 8 + y * 2, 0:128, :].astype(jnp.float32)
                right = ref[xh * 8 + y * 2 + 1, 0:128, :].astype(jnp.float32)
                real = jnp.where(low, left, pltpu.roll(right, 64, 1))
                imag = jnp.where(low, pltpu.roll(left, 64, 1), right)
                cosine = phase_cos[y, pl.ds(base, 128), :]
                sine = phase_sin[y, pl.ds(base, 128), :]
                spectrum[y, pl.ds(base, 128), :] = real * cosine - imag * sine
                spectrum[y, pl.ds(base + MASK_ROWS, 128), :] = real * sine + imag * cosine
    spectrum[4, :, :] = jnp.zeros((2 * MASK_ROWS, 128), jnp.float32)

    plus[...] = jnp.zeros_like(plus)
    minus[...] = jnp.zeros_like(minus)
    edges[...] = jnp.zeros_like(edges)
    sublane_lane = iota((16, 128), 1)
    lane = iota((PASS, 128), 1)
    fold_lane = iota((2 * SPAN, 128), 1)

    def row_transform(index, lhs, members=range(BATCH)):
        for u in members:
            code = order[index * BATCH + u]
            a = code & (COLUMN_UNIT - 1)
            b = (code >> 9) & (COLUMN_UNIT - 1)
            tile = b >> 7
            offset = b & 127
            back = (128 - offset) & 127
            before = (sublane_lane < offset).astype(jnp.bfloat16)
            left, right = [pltpu.roll(pupil[h], offset, 1).reshape(16, 16, 128) for h in range(2)]
            change = before * (left - right)
            masks = [(left - change).reshape(PASS, 128), (right + change).reshape(PASS, 128)]
            turned = []
            for t in range(2):
                window = []
                for part in range(2):
                    rows = pl.ds(a + part * MASK_ROWS, PASS)
                    piece = spectrum[tile + t, rows, :]
                    if t == 0:
                        piece = jnp.where(lane < offset, spectrum[tile + 2, rows, :], piece)
                    window.append(piece.astype(jnp.bfloat16) * masks[t])
                pair = jnp.dot(row_table[code >> 18], jnp.concatenate(window, axis=1), preferred_element_type=jnp.float32)
                rows = []
                for g in range(SPAN // 8):
                    first, second = (8 * (g & 3), 32 + 8 * (g & 3)) if g < 8 else (64, 72)
                    cos_re, sin_re = pair[first : first + 8, 0:128], pair[second : second + 8, 0:128]
                    cos_im, sin_im = pair[first : first + 8, 128:256], pair[second : second + 8, 128:256]
                    rows += [cos_re + sin_im, cos_im - sin_re] if 4 <= g < 8 else [cos_re - sin_im, cos_im + sin_re]
                turned.append(jnp.concatenate(rows, axis=0))
            inside = fold_lane >= offset
            for t in range(2):
                lhs[u * 2 * SPAN : (u + 1) * 2 * SPAN, t * 128 : (t + 1) * 128] = pltpu.roll(
                    jnp.where(inside, turned[t], turned[1 - t]).astype(jnp.bfloat16), back, 1
                )

    def column_transform(index, lhs, members=range(BATCH)):
        span = slice(members[0] * 2 * SPAN, (members[-1] + 1) * 2 * SPAN)
        field = jnp.dot(lhs[span, :], col_table[...], preferred_element_type=jnp.float32)
        for g in range(SPAN // 8):
            here = slice(8 * g, 8 * g + 8)
            sums = [plus[here, :], minus[here, :], edges[here, :]]
            for u in range(len(members)):
                first = u * 2 * SPAN + 16 * g
                real, imag = field[first : first + 8], field[first + 8 : first + 16]
                cos_re, sin_re, cos_im, sin_im = real[:, 0:128], real[:, 128:256], imag[:, 0:128], imag[:, 128:256]
                right_re, right_im = cos_re - sin_im, cos_im + sin_re
                left_re, left_im = cos_re + sin_im, cos_im - sin_re
                edge_re, edge_im = real[:, 256:384] - imag[:, 384:512], imag[:, 256:384] + real[:, 384:512]
                sums[0] = sums[0] + (right_re * right_re + right_im * right_im)
                sums[1] = sums[1] + (left_re * left_re + left_im * left_im)
                sums[2] = sums[2] + (edge_re * edge_re + edge_im * edge_im)
            plus[here, :], minus[here, :], edges[here, :] = sums

    row_transform(0, lhs_even)

    def two_batches(index, carry):
        half = BATCH // 2
        for old, new, step in ((lhs_even, lhs_odd, 0), (lhs_odd, lhs_even, 1)):
            for part in (range(half), range(half, BATCH)):
                column_transform(2 * index + step, old, part)
                row_transform(2 * index + step + 1, new, part)
        return carry

    batches = jnp.maximum((count + BATCH - 1) // BATCH, 1)
    whole = (batches - 1) // 2
    lax.fori_loop(0, whole, two_batches, 0)
    column_transform(2 * whole, lhs_even)

    @pl.when(2 * whole + 1 < batches)
    def last_batch():
        row_transform(2 * whole + 1, lhs_odd)
        column_transform(2 * whole + 1, lhs_odd)

    def place_by(left, right):
        return jnp.dot(left, right, precision=lax.Precision.HIGHEST, preferred_element_type=jnp.float32)

    source, target = iota((128, 128), 0), iota((128, 128), 1)
    mirror = (source + target == 127).astype(jnp.float32)
    beyond = ((source == target) & (source < 2)) | ((source + target == 129) & (source >= 2) & (source < 4))
    folded = jnp.concatenate(
        [place_by(minus[...], mirror), plus[...], place_by(edges[...], beyond.astype(jnp.float32))], axis=1
    )
    target, source = iota((SPAN, SPAN), 0), iota((SPAN, SPAN), 1)
    wanted = jnp.where(
        target < 32, 63 - target, jnp.where(target < 64, target - 32, jnp.where(target < 68, target, 137 - target))
    )
    intensity = place_by((source == wanted).astype(jnp.float32), folded) * (1.0 / (2 * SOURCES))

    shape = (SPAN, COLS + 128)
    line = iota(shape, 0)
    line = row0 + jnp.where(line < 66, line, line - SPAN)
    pixel = iota(shape, 1)
    pixel = col0 + jnp.where(pixel < COLS + 64, pixel, pixel - (COLS + 128))
    inside = (line >= 0) & (line < FRAME) & (pixel >= 0) & (pixel < FRAME)
    level = jnp.where(inside, 1.0 - jnp.exp(-intensity), 0.0)
    for repeat in range(2):
        beside = (
            pltpu.roll(level, SPAN - 1, 0)
            + pltpu.roll(level, 1, 0)
            + pltpu.roll(level, COLS + 127, 1)
            + pltpu.roll(level, 1, 1)
        )
        level = jnp.where(inside, level + DIFFUSION * (beside - 4.0 * level), 0.0)
    out_ref[...] = level[0:ROWS, 0:COLS]


VMEM_SPEC = pl.BlockSpec(memory_space=pltpu.VMEM)
SMEM_SPEC = pl.BlockSpec(memory_space=pltpu.SMEM)


def make_tables(place, pupil_mask):
    return pl.pallas_call(
        tables_kernel,
        out_shape=(
            jax.ShapeDtypeStruct((TOP_WEIGHT + 1, TABLE_ROWS, PASS), jnp.bfloat16),
            jax.ShapeDtypeStruct((PASS, 512), jnp.bfloat16),
            jax.ShapeDtypeStruct((3, PASS, 128), jnp.bfloat16),
            jax.ShapeDtypeStruct((4, MASK_ROWS, 128), jnp.float32),
            jax.ShapeDtypeStruct((4, MASK_ROWS, 128), jnp.float32),
        ),
        in_specs=[SMEM_SPEC, VMEM_SPEC],
        out_specs=(VMEM_SPEC,) * 5,
        compiler_params=pltpu.CompilerParams(vmem_limit_bytes=16 << 20),
        cost_estimate=pl.CostEstimate(flops=8_000_000, bytes_accessed=3_000_000, transcendentals=0),
    )(place, pupil_mask)


def image_block(place, codes, own, other, tables):
    return pl.pallas_call(
        image_kernel,
        out_shape=jax.ShapeDtypeStruct((ROWS, COLS), jnp.float32),
        in_specs=[SMEM_SPEC, SMEM_SPEC] + [VMEM_SPEC] * 7,
        out_specs=VMEM_SPEC,
        scratch_shapes=[
            pltpu.VMEM((5, 2 * MASK_ROWS, 128), jnp.float32),
            pltpu.VMEM((BATCH * 2 * SPAN, PASS), jnp.bfloat16),
            pltpu.VMEM((BATCH * 2 * SPAN, PASS), jnp.bfloat16),
            pltpu.VMEM((SPAN, 128), jnp.float32),
            pltpu.VMEM((SPAN, 128), jnp.float32),
            pltpu.VMEM((SPAN, 128), jnp.float32),
            pltpu.SMEM((SOURCES + 4 * BATCH,), jnp.int32),
        ],
        compiler_params=pltpu.CompilerParams(vmem_limit_bytes=32 << 20),
    )(place, codes, own, other, *tables)


def spread_block_kernel(spectrum_ref, out_ref):
    block = jnp.concatenate([spectrum_ref[0], spectrum_ref[1]], axis=1)
    for peer in range(out_ref.shape[0]):
        out_ref[peer] = block


def spread_column_kernel(column_ref, numbers_ref, out_ref):
    rows = column_ref.shape[0]
    for peer in range(out_ref.shape[0]):
        out_ref[peer, 0:rows, :] = column_ref[...]
        out_ref[peer, rows:, :] = numbers_ref[...]


def spread(kernel, shape, limit, *blocks):
    return pl.pallas_call(
        kernel,
        out_shape=jax.ShapeDtypeStruct(shape, jnp.bfloat16),
        in_specs=[VMEM_SPEC] * len(blocks),
        out_specs=VMEM_SPEC,
        compiler_params=pltpu.CompilerParams(vmem_limit_bytes=limit),
    )(*blocks)


def swap_blocks(copies, axes):
    return lax.all_to_all(copies, axes, 0, 0, tiled=True)


def body(spectrum, pupil_mask, source_shifts, source_weights):
    column = swap_blocks(spread(spread_block_kernel, (8, 16, 128), 32 << 20, spectrum), ("z",)).reshape(128, 128)
    numbers = jnp.concatenate([source_shifts.T, source_weights[None]], axis=0)
    numbers = jnp.pad(numbers, ((0, 5), (0, 96))).astype(jnp.bfloat16)
    own = swap_blocks(spread(spread_column_kernel, (16, 136, 128), 4 << 20, column, numbers), ("xh", "y", "xl"))
    other = lax.ppermute(own, "core", [(0, 1), (1, 0)])
    listed = own[0:8, 128:136, 0:32].astype(jnp.int32)
    codes = listed[:, 0] + COLUMN_UNIT * listed[:, 1] + WEIGHT_UNIT * listed[:, 2]
    core = lax.axis_index("core")
    tile = 2 * lax.axis_index("xh") + core
    group = 2 * lax.axis_index("y") + lax.axis_index("xl")
    place = jnp.stack([tile * 512 + group * ROWS, lax.axis_index("z") * COLS, core])
    return image_block(place, codes, own, other, make_tables(place, pupil_mask))


def solution(mesh):
    fine = Mesh(np.asarray(mesh.devices).reshape(2, 2, 8, 4, 2), ("xh", "core", "z", "y", "xl"))
    tx, ty, src = ("xh", "core"), "z", ("y", "xl")
    placed = (P(None, (*tx, ty), src), P(), P(src, None), P(src))
    return jax.shard_map(
        body, mesh=fine, in_specs=placed, out_specs=P((*tx, *src), ty), check_vma=False
    )
```

```python
import jax
import jax.numpy as jnp
import numpy as np
from jax import lax
from jax.experimental import pallas as pl
from jax.experimental.pallas import tpu as pltpu
from jax.sharding import Mesh
from jax.sharding import PartitionSpec as P

FRAME = 2048
TURN = 2 * FRAME
PASS = 256
MASK_ROWS = 512
SOURCES = 256
ROWS = 64
COLS = 256
SPAN = 72
TABLE_ROWS = 80
BATCH = 4
TOP_WEIGHT = 8
WEIGHT_UNIT = 1 << 18
COLUMN_UNIT = 1 << 9
DIFFUSION = 0.2


def turn_cos_sin(turns):
    shifted = turns + TURN // 8
    quadrant = (shifted >> 10) & 3
    angle = ((shifted & 1023) - TURN // 8).astype(jnp.float32) * (2.0 * jnp.pi / TURN)
    square = angle * angle
    sine = angle * (
        1.0 + square * (-1.0 / 6 + square * (1.0 / 120 + square * (-1.0 / 5040 + square * (1.0 / 362880))))
    )
    cosine = 1.0 + square * (-0.5 + square * (1.0 / 24 + square * (-1.0 / 720 + square * (1.0 / 40320))))
    odd = (quadrant & 1) == 1
    cos_part = jnp.where(odd, sine, cosine)
    sin_part = jnp.where(odd, cosine, sine)
    cos_part = jnp.where((quadrant == 1) | (quadrant == 2), -cos_part, cos_part)
    sin_part = jnp.where(quadrant >= 2, -sin_part, sin_part)
    return cos_part, sin_part


def iota(shape, dim):
    return lax.broadcasted_iota(jnp.int32, shape, dim)


def tables_kernel(place_ref, pupil_ref, row_table, col_table, pupil, phase_cos, phase_sin):
    whole = pupil_ref[...].astype(jnp.float32)
    for part, half in enumerate((whole[:, 0:128], whole[:, 128:256], whole[:, 0:128] - whole[:, 128:256])):
        pupil[part] = half.astype(jnp.bfloat16)

    shape = (TABLE_ROWS, PASS)
    line = iota(shape, 0)
    is_sin = ((line >= 32) & (line < 64)) | (line >= 72)
    pair = jnp.where(line < 64, line & 31, 32 + (line & 1))
    cosine, sine = turn_cos_sin((2 * pair + 1) * (iota(shape, 1) - PASS // 2))
    wave = jnp.where(is_sin, jnp.where((line >= 64) & ((line & 2) == 2), -sine, sine), cosine)
    for weight in range(TOP_WEIGHT + 1):
        row_table[weight] = (weight**0.5 * wave).astype(jnp.bfloat16)

    shape = (PASS, 128)
    frequency = iota(shape, 0) - PASS // 2
    lane = iota(shape, 1)
    cosine, sine = turn_cos_sin((2 * lane + 1) * frequency)
    col_table[:, 0:128] = cosine.astype(jnp.bfloat16)
    col_table[:, 128:256] = sine.astype(jnp.bfloat16)
    cosine, sine = turn_cos_sin((2 * (128 + (lane & 1)) + 1) * frequency)
    col_table[:, 256:384] = cosine.astype(jnp.bfloat16)
    col_table[:, 384:512] = jnp.where((lane & 2) == 0, sine, -sine).astype(jnp.bfloat16)

    row_turns = 2 * place_ref[0] + ROWS - 1
    col_turns = 2 * place_ref[1] + COLS - 1
    shape = (MASK_ROWS, 128)
    row_cos, row_sin = turn_cos_sin(row_turns * iota(shape, 0))
    for tile in range(4):
        col_cos, col_sin = turn_cos_sin(col_turns * (iota((8, 128), 1) + 128 * tile))
        col_cos, col_sin = col_cos[0:1], col_sin[0:1]
        phase_cos[tile] = row_cos * col_cos - row_sin * col_sin
        phase_sin[tile] = row_sin * col_cos + row_cos * col_sin


def image_kernel(
    place_ref, codes_ref, own_ref, other_ref, row_table, col_table, pupil, phase_cos, phase_sin, out_ref,
    spectrum, lhs_even, lhs_odd, plus, minus, edges, order,
):
    row0 = place_ref[0]
    col0 = place_ref[1]
    core = place_ref[2]

    count = jnp.int32(0)
    for s in range(SOURCES):
        code = codes_ref[s // 32, s % 32]
        order[count] = code
        count = count + (code >= WEIGHT_UNIT).astype(jnp.int32)
    for s in range(3 * BATCH):
        order[count + s] = jnp.int32(0)

    low = iota((128, 128), 1) < 64
    for half, ref in ((core, own_ref), (1 - core, other_ref)):
        for xh in range(2):
            base = pl.multiple_of((2 * xh + half) * 128, 128)
            for y in range(4):
                left = ref[xh * 8 + y * 2, 0:128, :].astype(jnp.float32)
                right = ref[xh * 8 + y * 2 + 1, 0:128, :].astype(jnp.float32)
                real = jnp.where(low, left, pltpu.roll(right, 64, 1))
                imag = jnp.where(low, pltpu.roll(left, 64, 1), right)
                cosine = phase_cos[y, pl.ds(base, 128), :]
                sine = phase_sin[y, pl.ds(base, 128), :]
                spectrum[y, pl.ds(base, 128), :] = real * cosine - imag * sine
                spectrum[y, pl.ds(base + MASK_ROWS, 128), :] = real * sine + imag * cosine
    spectrum[4, :, :] = jnp.zeros((2 * MASK_ROWS, 128), jnp.float32)

    plus[...] = jnp.zeros_like(plus)
    minus[...] = jnp.zeros_like(minus)
    edges[...] = jnp.zeros_like(edges)
    sublane_lane = iota((16, 128), 1)
    lane = iota((PASS, 128), 1)
    fold_lane = iota((2 * SPAN, 128), 1)

    def row_transform(index, lhs, members=range(BATCH)):
        for u in members:
            code = order[index * BATCH + u]
            a = code & (COLUMN_UNIT - 1)
            b = (code >> 9) & (COLUMN_UNIT - 1)
            tile = b >> 7
            offset = b & 127
            back = (128 - offset) & 127
            before = (sublane_lane < offset).astype(jnp.bfloat16)
            left, right = [pltpu.roll(pupil[h], offset, 1).reshape(16, 16, 128) for h in range(2)]
            change = before * (left - right)
            masks = [(left - change).reshape(PASS, 128), (right + change).reshape(PASS, 128)]
            turned = []
            for t in range(2):
                window = []
                for part in range(2):
                    rows = pl.ds(a + part * MASK_ROWS, PASS)
                    piece = spectrum[tile + t, rows, :]
                    if t == 0:
                        piece = jnp.where(lane < offset, spectrum[tile + 2, rows, :], piece)
                    window.append(piece.astype(jnp.bfloat16) * masks[t])
                pair = jnp.dot(row_table[code >> 18], jnp.concatenate(window, axis=1), preferred_element_type=jnp.float32)
                rows = []
                for g in range(SPAN // 8):
                    first, second = (8 * (g & 3), 32 + 8 * (g & 3)) if g < 8 else (64, 72)
                    cos_re, sin_re = pair[first : first + 8, 0:128], pair[second : second + 8, 0:128]
                    cos_im, sin_im = pair[first : first + 8, 128:256], pair[second : second + 8, 128:256]
                    rows += [cos_re + sin_im, cos_im - sin_re] if 4 <= g < 8 else [cos_re - sin_im, cos_im + sin_re]
                turned.append(jnp.concatenate(rows, axis=0))
            inside = fold_lane >= offset
            for t in range(2):
                lhs[u * 2 * SPAN : (u + 1) * 2 * SPAN, t * 128 : (t + 1) * 128] = pltpu.roll(
                    jnp.where(inside, turned[t], turned[1 - t]).astype(jnp.bfloat16), back, 1
                )

    def column_transform(index, lhs, members=range(BATCH)):
        span = slice(members[0] * 2 * SPAN, (members[-1] + 1) * 2 * SPAN)
        field = jnp.dot(lhs[span, :], col_table[...], preferred_element_type=jnp.float32)
        for g in range(SPAN // 8):
            here = slice(8 * g, 8 * g + 8)
            sums = [plus[here, :], minus[here, :], edges[here, :]]
            for u in range(len(members)):
                first = u * 2 * SPAN + 16 * g
                real, imag = field[first : first + 8], field[first + 8 : first + 16]
                cos_re, sin_re, cos_im, sin_im = real[:, 0:128], real[:, 128:256], imag[:, 0:128], imag[:, 128:256]
                right_re, right_im = cos_re - sin_im, cos_im + sin_re
                left_re, left_im = cos_re + sin_im, cos_im - sin_re
                edge_re, edge_im = real[:, 256:384] - imag[:, 384:512], imag[:, 256:384] + real[:, 384:512]
                sums[0] = sums[0] + (right_re * right_re + right_im * right_im)
                sums[1] = sums[1] + (left_re * left_re + left_im * left_im)
                sums[2] = sums[2] + (edge_re * edge_re + edge_im * edge_im)
            plus[here, :], minus[here, :], edges[here, :] = sums

    row_transform(0, lhs_even)

    def two_batches(first):
        half = BATCH // 2
        for old, new, step in ((lhs_even, lhs_odd, 0), (lhs_odd, lhs_even, 1)):
            for part in (range(half), range(half, BATCH)):
                column_transform(first + step, old, part)
                row_transform(first + step + 1, new, part)

    def four_batches(index, carry):
        two_batches(4 * index)
        two_batches(4 * index + 2)
        return carry

    batches = jnp.maximum((count + BATCH - 1) // BATCH, 1)
    whole = (batches - 1) // 2
    lax.fori_loop(0, whole // 2, four_batches, 0)

    @pl.when(whole % 2 == 1)
    def odd_pair():
        two_batches(2 * whole - 2)

    column_transform(2 * whole, lhs_even)

    @pl.when(2 * whole + 1 < batches)
    def last_batch():
        row_transform(2 * whole + 1, lhs_odd)
        column_transform(2 * whole + 1, lhs_odd)

    def split(values):
        parts = []
        for _ in range(3):
            parts.append(values.astype(jnp.bfloat16))
            values = values - parts[-1].astype(jnp.float32)
        return parts

    def dot(left, right):
        return jnp.dot(left, right, preferred_element_type=jnp.float32)

    def columns_by(values, choice):
        return sum(dot(part, choice.astype(jnp.bfloat16)) for part in split(values))

    def rows_by(choice, values):
        return sum(dot(choice.astype(jnp.bfloat16), part) for part in split(values))

    source, target = iota((128, 128), 0), iota((128, 128), 1)
    mirror = (source + target == 127).astype(jnp.float32)
    beyond = ((source == target) & (source < 2)) | ((source + target == 129) & (source >= 2) & (source < 4))
    folded = jnp.concatenate(
        [columns_by(minus[...], mirror), plus[...], columns_by(edges[...], beyond.astype(jnp.float32))], axis=1
    )
    target, source = iota((SPAN, SPAN), 0), iota((SPAN, SPAN), 1)
    wanted = jnp.where(
        target < 32, 63 - target, jnp.where(target < 64, target - 32, jnp.where(target < 68, target, 137 - target))
    )
    intensity = rows_by((source == wanted).astype(jnp.float32), folded) * (1.0 / (2 * SOURCES))

    shape = (SPAN, COLS + 128)
    line = iota(shape, 0)
    line = row0 + jnp.where(line < 66, line, line - SPAN)
    pixel = iota(shape, 1)
    pixel = col0 + jnp.where(pixel < COLS + 64, pixel, pixel - (COLS + 128))
    inside = (line >= 0) & (line < FRAME) & (pixel >= 0) & (pixel < FRAME)
    level = jnp.where(inside, 1.0 - jnp.exp(-intensity), 0.0)
    for repeat in range(2):
        beside = (
            pltpu.roll(level, SPAN - 1, 0)
            + pltpu.roll(level, 1, 0)
            + pltpu.roll(level, COLS + 127, 1)
            + pltpu.roll(level, 1, 1)
        )
        level = jnp.where(inside, level + DIFFUSION * (beside - 4.0 * level), 0.0)
    out_ref[...] = level[0:ROWS, 0:COLS]


VMEM_SPEC = pl.BlockSpec(memory_space=pltpu.VMEM)
SMEM_SPEC = pl.BlockSpec(memory_space=pltpu.SMEM)


def make_tables(place, pupil_mask):
    return pl.pallas_call(
        tables_kernel,
        out_shape=(
            jax.ShapeDtypeStruct((TOP_WEIGHT + 1, TABLE_ROWS, PASS), jnp.bfloat16),
            jax.ShapeDtypeStruct((PASS, 512), jnp.bfloat16),
            jax.ShapeDtypeStruct((3, PASS, 128), jnp.bfloat16),
            jax.ShapeDtypeStruct((4, MASK_ROWS, 128), jnp.float32),
            jax.ShapeDtypeStruct((4, MASK_ROWS, 128), jnp.float32),
        ),
        in_specs=[SMEM_SPEC, VMEM_SPEC],
        out_specs=(VMEM_SPEC,) * 5,
        compiler_params=pltpu.CompilerParams(vmem_limit_bytes=16 << 20),
        cost_estimate=pl.CostEstimate(flops=8_000_000, bytes_accessed=3_000_000, transcendentals=0),
    )(place, pupil_mask)


def image_block(place, codes, own, other, tables):
    return pl.pallas_call(
        image_kernel,
        out_shape=jax.ShapeDtypeStruct((ROWS, COLS), jnp.float32),
        in_specs=[SMEM_SPEC, SMEM_SPEC] + [VMEM_SPEC] * 7,
        out_specs=VMEM_SPEC,
        scratch_shapes=[
            pltpu.VMEM((5, 2 * MASK_ROWS, 128), jnp.float32),
            pltpu.VMEM((BATCH * 2 * SPAN, PASS), jnp.bfloat16),
            pltpu.VMEM((BATCH * 2 * SPAN, PASS), jnp.bfloat16),
            pltpu.VMEM((SPAN, 128), jnp.float32),
            pltpu.VMEM((SPAN, 128), jnp.float32),
            pltpu.VMEM((SPAN, 128), jnp.float32),
            pltpu.SMEM((SOURCES + 4 * BATCH,), jnp.int32),
        ],
        compiler_params=pltpu.CompilerParams(vmem_limit_bytes=32 << 20),
    )(place, codes, own, other, *tables)


def gather_blocks(block, axes, count):
    copies = jnp.broadcast_to(block[None], (count,) + block.shape)
    return lax.all_to_all(copies, axes, 0, 0, tiled=True)


def body(spectrum, pupil_mask, source_shifts, source_weights):
    block = jnp.concatenate([spectrum[0], spectrum[1]], axis=1)
    column = gather_blocks(block, ("z",), 8).reshape(128, 128)
    numbers = jnp.concatenate([source_shifts.T, source_weights[None]], axis=0)
    numbers = jnp.pad(numbers, ((0, 5), (0, 96))).astype(jnp.bfloat16)
    own = gather_blocks(jnp.concatenate([column, numbers], axis=0), ("xh", "y", "xl"), 16)
    other = lax.ppermute(own, "core", [(0, 1), (1, 0)])
    listed = own[0:8, 128:136, 0:32].astype(jnp.int32)
    codes = listed[:, 0] + COLUMN_UNIT * listed[:, 1] + WEIGHT_UNIT * listed[:, 2]
    core = lax.axis_index("core")
    tile = 2 * lax.axis_index("xh") + core
    group = 2 * lax.axis_index("y") + lax.axis_index("xl")
    place = jnp.stack([tile * 512 + group * ROWS, lax.axis_index("z") * COLS, core])
    return image_block(place, codes, own, other, make_tables(place, pupil_mask))


def solution(mesh):
    fine = Mesh(np.asarray(mesh.devices).reshape(2, 2, 8, 4, 2), ("xh", "core", "z", "y", "xl"))
    tx, ty, src = ("xh", "core"), "z", ("y", "xl")
    placed = (P(None, (*tx, ty), src), P(), P(src, None), P(src))
    return jax.shard_map(
        body, mesh=fine, in_specs=placed, out_specs=P((*tx, *src), ty), check_vma=False
    )
```

```python
import jax
import jax.numpy as jnp
import numpy as np
from jax import lax
from jax.experimental import pallas as pl
from jax.experimental.pallas import tpu as pltpu
from jax.sharding import Mesh
from jax.sharding import PartitionSpec as P

FRAME = 2048
TURN = 2 * FRAME
PASS = 256
MASK_ROWS = 512
SOURCES = 256
ROWS = 64
COLS = 256
SPAN = 72
TABLE_ROWS = 80
BATCH = 4
PAIRS = 3
TOP_WEIGHT = 8
WEIGHT_UNIT = 1 << 18
COLUMN_UNIT = 1 << 9
DIFFUSION = 0.2


def turn_cos_sin(turns):
    shifted = turns + TURN // 8
    quadrant = (shifted >> 10) & 3
    angle = ((shifted & 1023) - TURN // 8).astype(jnp.float32) * (2.0 * jnp.pi / TURN)
    square = angle * angle
    sine = angle * (
        1.0 + square * (-1.0 / 6 + square * (1.0 / 120 + square * (-1.0 / 5040 + square * (1.0 / 362880))))
    )
    cosine = 1.0 + square * (-0.5 + square * (1.0 / 24 + square * (-1.0 / 720 + square * (1.0 / 40320))))
    odd = (quadrant & 1) == 1
    cos_part = jnp.where(odd, sine, cosine)
    sin_part = jnp.where(odd, cosine, sine)
    cos_part = jnp.where((quadrant == 1) | (quadrant == 2), -cos_part, cos_part)
    sin_part = jnp.where(quadrant >= 2, -sin_part, sin_part)
    return cos_part, sin_part


def iota(shape, dim):
    return lax.broadcasted_iota(jnp.int32, shape, dim)


def tables_kernel(place_ref, pupil_ref, row_table, col_table, pupil, phase_cos, phase_sin):
    whole = pupil_ref[...].astype(jnp.float32)
    for part, half in enumerate((whole[:, 0:128], whole[:, 128:256], whole[:, 0:128] - whole[:, 128:256])):
        pupil[part] = half.astype(jnp.bfloat16)

    shape = (TABLE_ROWS, PASS)
    line = iota(shape, 0)
    is_sin = ((line >= 32) & (line < 64)) | (line >= 72)
    pair = jnp.where(line < 64, line & 31, 32 + (line & 1))
    cosine, sine = turn_cos_sin((2 * pair + 1) * (iota(shape, 1) - PASS // 2))
    wave = jnp.where(is_sin, jnp.where((line >= 64) & ((line & 2) == 2), -sine, sine), cosine)
    for weight in range(TOP_WEIGHT + 1):
        row_table[weight] = (weight**0.5 * wave).astype(jnp.bfloat16)

    shape = (PASS, 128)
    frequency = iota(shape, 0) - PASS // 2
    lane = iota(shape, 1)
    cosine, sine = turn_cos_sin((2 * lane + 1) * frequency)
    col_table[:, 0:128] = cosine.astype(jnp.bfloat16)
    col_table[:, 128:256] = sine.astype(jnp.bfloat16)
    cosine, sine = turn_cos_sin((2 * (128 + (lane & 1)) + 1) * frequency)
    col_table[:, 256:384] = cosine.astype(jnp.bfloat16)
    col_table[:, 384:512] = jnp.where((lane & 2) == 0, sine, -sine).astype(jnp.bfloat16)

    row_turns = 2 * place_ref[0] + ROWS - 1
    col_turns = 2 * place_ref[1] + COLS - 1
    shape = (MASK_ROWS, 128)
    row_cos, row_sin = turn_cos_sin(row_turns * iota(shape, 0))
    for tile in range(4):
        col_cos, col_sin = turn_cos_sin(col_turns * (iota((8, 128), 1) + 128 * tile))
        col_cos, col_sin = col_cos[0:1], col_sin[0:1]
        phase_cos[tile] = row_cos * col_cos - row_sin * col_sin
        phase_sin[tile] = row_sin * col_cos + row_cos * col_sin


def image_kernel(
    place_ref, codes_ref, own_ref, other_ref, row_table, col_table, pupil, phase_cos, phase_sin, out_ref,
    spectrum, lhs_even, lhs_odd, plus, minus, edges, order,
):
    row0 = place_ref[0]
    col0 = place_ref[1]
    core = place_ref[2]

    count = jnp.int32(0)
    for s in range(SOURCES):
        code = codes_ref[s // 32, s % 32]
        order[count] = code
        count = count + (code >= WEIGHT_UNIT).astype(jnp.int32)
    for s in range(3 * BATCH):
        order[count + s] = jnp.int32(0)

    low = iota((128, 128), 1) < 64
    for half, ref in ((core, own_ref), (1 - core, other_ref)):
        for xh in range(2):
            base = pl.multiple_of((2 * xh + half) * 128, 128)
            for y in range(4):
                left = ref[xh * 8 + y * 2, 0:128, :].astype(jnp.float32)
                right = ref[xh * 8 + y * 2 + 1, 0:128, :].astype(jnp.float32)
                real = jnp.where(low, left, pltpu.roll(right, 64, 1))
                imag = jnp.where(low, pltpu.roll(left, 64, 1), right)
                cosine = phase_cos[y, pl.ds(base, 128), :]
                sine = phase_sin[y, pl.ds(base, 128), :]
                spectrum[y, pl.ds(base, 128), :] = real * cosine - imag * sine
                spectrum[y, pl.ds(base + MASK_ROWS, 128), :] = real * sine + imag * cosine
    spectrum[4, :, :] = jnp.zeros((2 * MASK_ROWS, 128), jnp.float32)

    plus[...] = jnp.zeros_like(plus)
    minus[...] = jnp.zeros_like(minus)
    edges[...] = jnp.zeros_like(edges)
    sublane_lane = iota((16, 128), 1)
    lane = iota((PASS, 128), 1)
    fold_lane = iota((2 * SPAN, 128), 1)

    def row_transform(index, lhs, members=range(BATCH)):
        for u in members:
            code = order[index * BATCH + u]
            a = code & (COLUMN_UNIT - 1)
            b = (code >> 9) & (COLUMN_UNIT - 1)
            tile = b >> 7
            offset = b & 127
            back = (128 - offset) & 127
            before = (sublane_lane < offset).astype(jnp.bfloat16)
            left, right = [pltpu.roll(pupil[h], offset, 1).reshape(16, 16, 128) for h in range(2)]
            change = before * (left - right)
            masks = [(left - change).reshape(PASS, 128), (right + change).reshape(PASS, 128)]
            turned = []
            for t in range(2):
                window = []
                for part in range(2):
                    rows = pl.ds(a + part * MASK_ROWS, PASS)
                    piece = spectrum[tile + t, rows, :]
                    if t == 0:
                        piece = jnp.where(lane < offset, spectrum[tile + 2, rows, :], piece)
                    window.append(piece.astype(jnp.bfloat16) * masks[t])
                pair = jnp.dot(row_table[code >> 18], jnp.concatenate(window, axis=1), preferred_element_type=jnp.float32)
                rows = []
                for g in range(SPAN // 8):
                    first, second = (8 * (g & 3), 32 + 8 * (g & 3)) if g < 8 else (64, 72)
                    cos_re, sin_re = pair[first : first + 8, 0:128], pair[second : second + 8, 0:128]
                    cos_im, sin_im = pair[first : first + 8, 128:256], pair[second : second + 8, 128:256]
                    rows += [cos_re + sin_im, cos_im - sin_re] if 4 <= g < 8 else [cos_re - sin_im, cos_im + sin_re]
                turned.append(jnp.concatenate(rows, axis=0))
            inside = fold_lane >= offset
            for t in range(2):
                lhs[u * 2 * SPAN : (u + 1) * 2 * SPAN, t * 128 : (t + 1) * 128] = pltpu.roll(
                    jnp.where(inside, turned[t], turned[1 - t]).astype(jnp.bfloat16), back, 1
                )

    def column_transform(index, lhs, members=range(BATCH)):
        span = slice(members[0] * 2 * SPAN, (members[-1] + 1) * 2 * SPAN)
        field = jnp.dot(lhs[span, :], col_table[...], preferred_element_type=jnp.float32)
        for g in range(SPAN // 8):
            here = slice(8 * g, 8 * g + 8)
            sums = [plus[here, :], minus[here, :], edges[here, :]]
            for u in range(len(members)):
                first = u * 2 * SPAN + 16 * g
                real, imag = field[first : first + 8], field[first + 8 : first + 16]
                cos_re, sin_re, cos_im, sin_im = real[:, 0:128], real[:, 128:256], imag[:, 0:128], imag[:, 128:256]
                right_re, right_im = cos_re - sin_im, cos_im + sin_re
                left_re, left_im = cos_re + sin_im, cos_im - sin_re
                edge_re, edge_im = real[:, 256:384] - imag[:, 384:512], imag[:, 256:384] + real[:, 384:512]
                sums[0] = sums[0] + (right_re * right_re + right_im * right_im)
                sums[1] = sums[1] + (left_re * left_re + left_im * left_im)
                sums[2] = sums[2] + (edge_re * edge_re + edge_im * edge_im)
            plus[here, :], minus[here, :], edges[here, :] = sums

    row_transform(0, lhs_even)

    def two_batches(first):
        half = BATCH // 2
        for old, new, step in ((lhs_even, lhs_odd, 0), (lhs_odd, lhs_even, 1)):
            for part in (range(half), range(half, BATCH)):
                column_transform(first + step, old, part)
                row_transform(first + step + 1, new, part)

    def several_pairs(index, carry):
        for pair in range(PAIRS):
            two_batches(2 * (PAIRS * index + pair))
        return carry

    def one_pair(index, carry):
        two_batches(2 * index)
        return carry

    batches = jnp.maximum((count + BATCH - 1) // BATCH, 1)
    whole = (batches - 1) // 2
    turns = whole // PAIRS
    lax.fori_loop(0, turns, several_pairs, 0)
    lax.fori_loop(PAIRS * turns, whole, one_pair, 0)

    column_transform(2 * whole, lhs_even)

    @pl.when(2 * whole + 1 < batches)
    def last_batch():
        row_transform(2 * whole + 1, lhs_odd)
        column_transform(2 * whole + 1, lhs_odd)

    def split(values):
        parts = []
        for _ in range(3):
            parts.append(values.astype(jnp.bfloat16))
            values = values - parts[-1].astype(jnp.float32)
        return parts

    def dot(left, right):
        return jnp.dot(left, right, preferred_element_type=jnp.float32)

    def columns_by(values, choice):
        return sum(dot(part, choice.astype(jnp.bfloat16)) for part in split(values))

    def rows_by(choice, values):
        return sum(dot(choice.astype(jnp.bfloat16), part) for part in split(values))

    source, target = iota((128, 128), 0), iota((128, 128), 1)
    mirror = (source + target == 127).astype(jnp.float32)
    beyond = ((source == target) & (source < 2)) | ((source + target == 129) & (source >= 2) & (source < 4))
    folded = jnp.concatenate(
        [columns_by(minus[...], mirror), plus[...], columns_by(edges[...], beyond.astype(jnp.float32))], axis=1
    )
    target, source = iota((SPAN, SPAN), 0), iota((SPAN, SPAN), 1)
    wanted = jnp.where(
        target < 32, 63 - target, jnp.where(target < 64, target - 32, jnp.where(target < 68, target, 137 - target))
    )
    intensity = rows_by((source == wanted).astype(jnp.float32), folded) * (1.0 / (2 * SOURCES))

    shape = (SPAN, COLS + 128)
    line = iota(shape, 0)
    line = row0 + jnp.where(line < 66, line, line - SPAN)
    pixel = iota(shape, 1)
    pixel = col0 + jnp.where(pixel < COLS + 64, pixel, pixel - (COLS + 128))
    inside = (line >= 0) & (line < FRAME) & (pixel >= 0) & (pixel < FRAME)
    level = jnp.where(inside, 1.0 - jnp.exp(-intensity), 0.0)
    for repeat in range(2):
        beside = (
            pltpu.roll(level, SPAN - 1, 0)
            + pltpu.roll(level, 1, 0)
            + pltpu.roll(level, COLS + 127, 1)
            + pltpu.roll(level, 1, 1)
        )
        level = jnp.where(inside, level + DIFFUSION * (beside - 4.0 * level), 0.0)
    out_ref[...] = level[0:ROWS, 0:COLS]


VMEM_SPEC = pl.BlockSpec(memory_space=pltpu.VMEM)
SMEM_SPEC = pl.BlockSpec(memory_space=pltpu.SMEM)


def make_tables(place, pupil_mask):
    return pl.pallas_call(
        tables_kernel,
        out_shape=(
            jax.ShapeDtypeStruct((TOP_WEIGHT + 1, TABLE_ROWS, PASS), jnp.bfloat16),
            jax.ShapeDtypeStruct((PASS, 512), jnp.bfloat16),
            jax.ShapeDtypeStruct((3, PASS, 128), jnp.bfloat16),
            jax.ShapeDtypeStruct((4, MASK_ROWS, 128), jnp.float32),
            jax.ShapeDtypeStruct((4, MASK_ROWS, 128), jnp.float32),
        ),
        in_specs=[SMEM_SPEC, VMEM_SPEC],
        out_specs=(VMEM_SPEC,) * 5,
        compiler_params=pltpu.CompilerParams(vmem_limit_bytes=16 << 20),
        cost_estimate=pl.CostEstimate(flops=8_000_000, bytes_accessed=3_000_000, transcendentals=0),
    )(place, pupil_mask)


def image_block(place, codes, own, other, tables):
    return pl.pallas_call(
        image_kernel,
        out_shape=jax.ShapeDtypeStruct((ROWS, COLS), jnp.float32),
        in_specs=[SMEM_SPEC, SMEM_SPEC] + [VMEM_SPEC] * 7,
        out_specs=VMEM_SPEC,
        scratch_shapes=[
            pltpu.VMEM((5, 2 * MASK_ROWS, 128), jnp.float32),
            pltpu.VMEM((BATCH * 2 * SPAN, PASS), jnp.bfloat16),
            pltpu.VMEM((BATCH * 2 * SPAN, PASS), jnp.bfloat16),
            pltpu.VMEM((SPAN, 128), jnp.float32),
            pltpu.VMEM((SPAN, 128), jnp.float32),
            pltpu.VMEM((SPAN, 128), jnp.float32),
            pltpu.SMEM((SOURCES + 4 * BATCH,), jnp.int32),
        ],
        compiler_params=pltpu.CompilerParams(vmem_limit_bytes=32 << 20),
    )(place, codes, own, other, *tables)


def gather_blocks(block, axes, count):
    copies = jnp.broadcast_to(block[None], (count,) + block.shape)
    return lax.all_to_all(copies, axes, 0, 0, tiled=True)


def body(spectrum, pupil_mask, source_shifts, source_weights):
    block = jnp.concatenate([spectrum[0], spectrum[1]], axis=1)
    column = gather_blocks(block, ("z",), 8).reshape(128, 128)
    numbers = jnp.concatenate([source_shifts.T, source_weights[None]], axis=0)
    numbers = jnp.pad(numbers, ((0, 5), (0, 96))).astype(jnp.bfloat16)
    own = gather_blocks(jnp.concatenate([column, numbers], axis=0), ("xh", "y", "xl"), 16)
    other = lax.ppermute(own, "core", [(0, 1), (1, 0)])
    listed = own[0:8, 128:136, 0:32].astype(jnp.int32)
    codes = listed[:, 0] + COLUMN_UNIT * listed[:, 1] + WEIGHT_UNIT * listed[:, 2]
    core = lax.axis_index("core")
    tile = 2 * lax.axis_index("xh") + core
    group = 2 * lax.axis_index("y") + lax.axis_index("xl")
    place = jnp.stack([tile * 512 + group * ROWS, lax.axis_index("z") * COLS, core])
    return image_block(place, codes, own, other, make_tables(place, pupil_mask))


def solution(mesh):
    fine = Mesh(np.asarray(mesh.devices).reshape(2, 2, 8, 4, 2), ("xh", "core", "z", "y", "xl"))
    tx, ty, src = ("xh", "core"), "z", ("y", "xl")
    placed = (P(None, (*tx, ty), src), P(), P(src, None), P(src))
    return jax.shard_map(
        body, mesh=fine, in_specs=placed, out_specs=P((*tx, *src), ty), check_vma=False
    )
```
